32 devices in a mesh: grp: 2 (over x), view: 16 (over z, y, core).
Axes of the slice: x: 2, y: 2, z: 4, core: 2. Of those that a mesh axis runs over, the one named last changes fastest.
Arguments:
- features: float32 [32, 32, 8, 256], P(('grp', 'view')), parts along dimension 0, may hold values from -96 to 96, as said below
- offsets: int32 [32, 128], P(('grp', 'view')), parts along dimension 0, may hold values from 0 to 31
- conf_bins: int32 [16, 256], P('grp'), parts along dimension 0, may hold values from 0 to 3
- plane_depths: float32 [128], P('view'), may hold values from 1 to 10
Outputs:
- cost_volume: float32 [128, 16, 256], P('view', 'grp'), parts along dimension 1
- depth_map: float32 [16, 256], P('grp'), parts along dimension 0
The draws below stay inside these ranges and needn't reach their ends.
There are 2 independent parts, one for each index of `grp`. The reference program is written for one: setup_inputs(seed, part) draws one part's arguments, and reference() takes and returns one part's arrays. A program takes and returns all parts, laid end to end along the dimension named above; an argument that names none is the same for every part. Nothing has to cross between parts.
Inputs may be any that keep to these rules, and one draw needn't show every extreme that they name: `features`: feature entries may be large on some rows.
All inputs are finite; a program needn't handle non-finite values.
Results may differ from the reference program's by a relative error of at most 0.0003.
Values sent between devices are 32-bit elements; how exact they have to be, the bound alone decides.
A program may use at most 128 MiB of HBM per device.

```python
import jax
import jax.numpy as jnp
from jax import lax

C = 32
W = 256
PLANES = 128
ROWS = 8
ITERS = 4
VIEWS = 16


def draw_features(key, part):
    first = jax.random.fold_in(key, 0)
    third = jax.random.fold_in(key, 7)
    fourth = jax.random.fold_in(key, 11)
    fifth = jax.random.fold_in(key, 13)
    sixth = jax.random.fold_in(key, 17)
    noise = jnp.clip(jax.random.normal(first, (VIEWS, C, ROWS, W), jnp.float32), -6.0, 6.0)
    level = jnp.clip(jax.random.normal(fifth, (C, ROWS, 1), jnp.float32), -4.0, 4.0)
    shared = jnp.clip(jax.random.normal(sixth, (C, ROWS, W), jnp.float32), -6.0, 6.0)
    values = 0.7 * (level + shared)[None] + 0.7 * noise
    chosen_row = jax.random.randint(third, (), 0, ROWS)
    strength = jax.random.uniform(fourth, (), jnp.float32, 14.0, 24.0)
    row_marks = (jnp.arange(ROWS, dtype=jnp.int32) == chosen_row).astype(jnp.float32)
    row_scale = 1.0 + (strength - 1.0) * row_marks
    values = values * row_scale[:, None]
    return jnp.clip(values, -96.0, 96.0)


def set_ends(drawn, own_key, least, high):
    longest = drawn.shape.index(max(drawn.shape))
    spots = []
    for shift in (0, 1):
        where = [jax.random.randint(jax.random.fold_in(own_key, axis), (), 0, length) for axis, length in enumerate(drawn.shape)]
        where[longest] = (where[longest] + shift) % drawn.shape[longest]
        spots.append(tuple(where))
    return drawn.at[spots[0]].set(least).at[spots[1]].set(high)


def level_of(rng, shape, pieces, least, top_value):
    factor_of = 1.0
    for axis_at, shards_of in pieces:
        draws = jax.random.uniform(jax.random.fold_in(jax.random.fold_in(rng, 6), axis_at), (shards_of,), jnp.float32, least / len(pieces), top_value / len(pieces))
        factor_of = factor_of * jnp.repeat(jnp.exp(draws), shape[axis_at] // shards_of).reshape((-1,) + (1,) * (len(shape) - 1 - axis_at))
    return factor_of


def setup_inputs(seed: int = 0, part: int = 0) -> dict:
    key_list = jax.random.split(jax.random.key(seed), 5)
    part_splits = jax.random.split(jax.random.fold_in(key_list[4], part), 5)
    return {
        "features": draw_features(jax.random.fold_in(jax.random.fold_in(key_list[4], part), 71), part),
        "offsets": set_ends(jax.random.randint(part_splits[1], (VIEWS, PLANES), 0, W // 8), jax.random.fold_in(part_splits[1], 1), 0, (W // 8) - 1).astype(jnp.int32),
        "conf_bins": set_ends(jax.random.randint(part_splits[2], (ROWS, W), 0, 4), jax.random.fold_in(part_splits[2], 1), 0, 3).astype(jnp.int32),
        "plane_depths": jnp.clip(1.0 + 9.0 * jax.random.uniform(key_list[3], (PLANES,), jnp.float32) ** level_of(key_list[3], (PLANES,), ((0, 16),), -0.2, 0.2), 1.0, 10.0),
    }


def warp_tile(tile, shift):
    pad = tile.shape[2] // 8
    padded = jnp.pad(tile, ((0, 0), (0, 0), (pad, 0)))
    return lax.dynamic_slice_in_dim(padded, (pad - shift).astype(jnp.int32), tile.shape[2], 2)


def reference(features, offsets, conf_bins, plane_depths):
    count = features.shape[0]

    def one_plane(shifts):
        warped = jax.vmap(warp_tile)(features, shifts)
        total = jnp.sum(warped, axis=0)
        square = jnp.sum(warped * warped, axis=0)
        mean = total / count
        return jnp.mean(square / count - mean * mean, axis=0)

    cost = lax.map(one_plane, jnp.transpose(offsets))
    conf = (conf_bins.astype(jnp.float32) + 1.0) * 0.25
    for step in range(ITERS):
        padded = jnp.pad(cost, 1)
        beside = padded[2:, 1:-1, 1:-1] + padded[:-2, 1:-1, 1:-1]
        beside = beside + padded[1:-1, 2:, 1:-1] + padded[1:-1, :-2, 1:-1]
        beside = beside + padded[1:-1, 1:-1, 2:] + padded[1:-1, 1:-1, :-2]
        cost = cost + 0.15 * conf * (beside - 6.0 * cost)
    logits = -cost
    peak = jnp.max(logits, axis=0)
    weights = jnp.exp(logits - peak)
    depth = jnp.sum(weights * plane_depths[:, None, None], axis=0) / jnp.sum(weights, axis=0)
    return cost, depth
```

```python
import functools

import jax
import jax.numpy as jnp
from jax import lax
from jax.experimental import pallas as pl
from jax.experimental.pallas import tpu as pltpu
from jax.sharding import PartitionSpec as P

ITERS = 4
LANES = 128
GROUP = 8


def shifted(x, amount, lane):
    if amount == 0:
        return x
    return jnp.where(lane >= amount, pltpu.roll(x, amount, 1), 0.0)


def kernel(
    n, feat_ref, off_ref, conf_ref, depth_ref, cost_ref, map_ref,
    xs, xr, offv, offs, table, sqs, spad, part, costs, stat_s, stat_r, res,
    local_sem, xs_send, xs_recv, off_send, off_recv, c_send, c_recv, s_send, s_recv, r_send, r_recv,
):
    _, chans, rows, width = feat_ref.shape
    planes = off_ref.shape[-1]
    owned = depth_ref.shape[0]
    groups = n // rows
    cg = chans // groups
    pad = width // 8
    halo = ITERS
    span = 2 * GROUP
    per_window = GROUP // owned
    windows = planes // GROUP
    blocks = windows + 1
    halves = width // LANES
    owners = rows * halves
    me = lax.axis_index("view")
    my_window = me // per_window

    for r in range(rows):
        line = feat_ref[0, :, r, :]
        for g in range(groups):
            xs[r * groups + g] = line[g * cg:(g + 1) * cg]
    offv[me] = off_ref[...]

    barrier = pltpu.get_barrier_semaphore()

    def greet(k, carry):
        pl.semaphore_signal(barrier, inc=1, device_id={"view": lax.rem(me + k, n)})
        return carry

    lax.fori_loop(1, n, greet, 0)
    pl.semaphore_wait(barrier, n - 1)

    def off_copy(slot, peer):
        return pltpu.make_async_remote_copy(
            src_ref=offv.at[slot], dst_ref=offv.at[slot], send_sem=off_send.at[peer],
            recv_sem=off_recv.at[slot], device_id={"view": peer})

    def feat_copy(slot, peer):
        return pltpu.make_async_remote_copy(
            src_ref=xs.at[peer], dst_ref=xr.at[slot], send_sem=xs_send.at[peer],
            recv_sem=xs_recv.at[slot], device_id={"view": peer})

    def send_feat(k, carry):
        peer = lax.rem(me + k, n)
        off_copy(me, peer).start()
        feat_copy(me, peer).start()
        return carry

    lax.fori_loop(1, n, send_feat, 0)

    lane = lax.broadcasted_iota(jnp.int32, (cg, width), 1)

    def build(view, x):
        for o in range(pad):
            table[view * pad + o] = shifted(x, o, lane)
        sqs[pl.ds(view, 1), :] = jnp.sum(x * x, axis=0, keepdims=True)

    build(me, xs[me])

    def receive(k, carry):
        source = lax.rem(me - k + n, n)
        feat_copy(source, source).wait_recv()
        off_copy(source, source).wait_recv()
        build(source, xr[source])
        return carry

    lax.fori_loop(1, n, receive, 0)

    to_scalar = pltpu.make_async_copy(offv, offs, local_sem)
    to_scalar.start()
    chosen = offv[:, 0, :]
    sq = sqs[...]
    lane_n = lax.broadcasted_iota(jnp.int32, (n, width), 1)
    hot = jnp.concatenate(
        [jnp.where(chosen == o, 1.0, 0.0) for o in range(pad)], axis=0)
    sq_all = jnp.concatenate([shifted(sq, o, lane_n) for o in range(pad)], axis=0)
    hot = hot.T.astype(jnp.bfloat16)
    high = sq_all.astype(jnp.bfloat16)
    rest = sq_all - high.astype(jnp.float32)
    mid = rest.astype(jnp.bfloat16)
    low = (rest - mid.astype(jnp.float32)).astype(jnp.bfloat16)
    square = jnp.zeros((planes, width), jnp.float32)
    for piece in (low, mid, high):
        square = square + jnp.dot(hot, piece, preferred_element_type=jnp.float32)
    spad[...] = jnp.zeros_like(spad)
    spad[halo:halo + planes, :] = square * (1.0 / (n * chans))
    to_scalar.wait()

    def cost_copy(slot, peer, window):
        first = pl.multiple_of(window * GROUP, GROUP)
        return pltpu.make_async_remote_copy(
            src_ref=part.at[pl.ds(first, span)], dst_ref=costs.at[slot],
            send_sem=c_send.at[peer], recv_sem=c_recv.at[slot], device_id={"view": peer})

    def block(k, carry):
        j = lax.rem(my_window + 1 + k, blocks)
        sums = []
        for i in range(GROUP):
            p = jnp.clip(j * GROUP + i - halo, 0, planes - 1)
            total = table[offs[0, 0, p]]
            for v in range(1, n):
                total = total + table[v * pad + offs[v, 0, p]]
            sums.append(jnp.sum(total * total, axis=0, keepdims=True))
        first = pl.multiple_of(j * GROUP, GROUP)
        part[pl.ds(first, GROUP), :] = (
            spad[pl.ds(first, GROUP), :]
            - jnp.concatenate(sums, axis=0) * (1.0 / (n * n * chans)))

        @pl.when(jnp.logical_and(k > 0, j > 0))
        def _():
            for m in range(per_window):
                peer = (j - 1) * per_window + m
                cost_copy(me, peer, j - 1).start()

        return carry

    lax.fori_loop(0, blocks, block, 0)
    if per_window > 1:
        for m in range(per_window):
            peer = my_window * per_window + m

            @pl.when(peer != me)
            def _():
                cost_copy(me, peer, my_window).start()

    costs[me] = part[pl.ds(pl.multiple_of(my_window * GROUP, GROUP), span), :]

    def take(k, carry):
        source = lax.rem(me - k + n, n)
        cost_copy(source, source, 0).wait_recv()
        return carry

    lax.fori_loop(1, n, take, 0)

    plane = my_window * GROUP - halo + lax.broadcasted_iota(jnp.int32, (span, width), 0)
    valid = jnp.logical_and(plane >= 0, plane < planes)
    col = lax.broadcasted_iota(jnp.int32, (span, width), 1)
    cost, rate = [], []
    for r in range(rows):
        total = costs[r * groups]
        for g in range(1, groups):
            total = total + costs[r * groups + g]
        cost.append(jnp.where(valid, total, 0.0))
        conf = (conf_ref[r:r + 1, :].astype(jnp.float32) + 1.0) * 0.25
        rate.append(jnp.where(valid, 0.15 * conf, 0.0))
    for step in range(ITERS):
        new = []
        for r in range(rows):
            c = cost[r]
            beside = pltpu.roll(c, 1, 0) + pltpu.roll(c, span - 1, 0)
            if r > 0:
                beside = beside + cost[r - 1]
            if r < rows - 1:
                beside = beside + cost[r + 1]
            beside = beside + jnp.where(col > 0, pltpu.roll(c, 1, 1), 0.0)
            beside = beside + jnp.where(col < width - 1, pltpu.roll(c, width - 1, 1), 0.0)
            new.append(c + rate[r] * (beside - 6.0 * c))
        cost = new

    index = lax.broadcasted_iota(jnp.int32, (owned, width), 0)
    depth = jnp.zeros((owned, width), jnp.float32)
    for i in range(owned):
        depth = jnp.where(index == i, depth_ref[i], depth)
    for r in range(rows):
        own = cost[r][halo:halo + owned]
        for m in range(1, per_window):
            first = halo + m * owned
            own = jnp.where(lax.rem(me, per_window) == m, cost[r][first:first + owned], own)
        cost_ref[:, r, :] = own
        peak = jnp.max(-own, axis=0, keepdims=True)
        weight = jnp.exp(-own - peak)
        soft = jnp.concatenate(
            [peak, jnp.sum(weight, axis=0, keepdims=True),
             jnp.sum(weight * depth, axis=0, keepdims=True)], axis=0)
        for h in range(halves):
            stat_s[r * halves + h] = soft[:, h * LANES:(h + 1) * LANES]

    def stat_copy(slot, peer):
        return pltpu.make_async_remote_copy(
            src_ref=stat_s.at[peer], dst_ref=stat_r.at[slot], send_sem=s_send.at[peer],
            recv_sem=s_recv.at[slot], device_id={"view": peer})

    def res_copy(slot, peer):
        return pltpu.make_async_remote_copy(
            src_ref=res.at[slot], dst_ref=res.at[slot], send_sem=r_send.at[peer],
            recv_sem=r_recv.at[slot], device_id={"view": peer})

    def send_stat(k, carry):
        peer = lax.rem(me + k, n)

        @pl.when(peer < owners)
        def _():
            stat_copy(me, peer).start()

        return carry

    lax.fori_loop(1, n, send_stat, 0)

    @pl.when(me < owners)
    def _():
        stat_r[me] = stat_s[me]

        def wait_stat(k, carry):
            source = lax.rem(me - k + n, n)
            stat_copy(source, me).wait_recv()
            return carry

        lax.fori_loop(1, n, wait_stat, 0)
        got = stat_r[...]
        top = jnp.max(got[:, 0, :], axis=0, keepdims=True)
        scale = jnp.exp(got[:, 0, :] - top)
        denom = jnp.sum(got[:, 1, :] * scale, axis=0, keepdims=True)
        numer = jnp.sum(got[:, 2, :] * scale, axis=0, keepdims=True)
        res[me] = numer / denom

        def send_res(k, carry):
            res_copy(me, lax.rem(me + k, n)).start()
            return carry

        lax.fori_loop(1, n, send_res, 0)

    def finish(k, carry):
        peer = lax.rem(me + k, n)
        feat_copy(me, peer).wait_send()
        off_copy(me, peer).wait_send()
        cost_copy(me, peer, 0).wait_send()

        @pl.when(peer < owners)
        def _():
            stat_copy(me, peer).wait_send()
            res_copy(peer, peer).wait_recv()

        @pl.when(me < owners)
        def _():
            res_copy(me, peer).wait_send()

        return carry

    lax.fori_loop(1, n, finish, 0)
    for r in range(rows):
        for h in range(halves):
            map_ref[r:r + 1, h * LANES:(h + 1) * LANES] = res[r * halves + h]


def per_device(features, offsets, conf_bins, plane_depths):
    n = lax.axis_size("view")
    _, chans, rows, width = features.shape
    planes = offsets.shape[-1]
    owned = plane_depths.shape[0]
    cg = chans * rows // n
    pad = width // 8
    owners = rows * width // LANES
    padded = planes + 2 * ITERS
    f32 = jnp.float32
    vmem = pl.BlockSpec(memory_space=pltpu.VMEM)
    dma = pltpu.SemaphoreType.DMA
    return pl.pallas_call(
        functools.partial(kernel, n),
        out_shape=(
            jax.ShapeDtypeStruct((owned, rows, width), f32),
            jax.ShapeDtypeStruct((rows, width), f32),
        ),
        in_specs=[vmem, vmem, vmem, pl.BlockSpec(memory_space=pltpu.SMEM)],
        out_specs=(vmem, vmem),
        scratch_shapes=[
            pltpu.VMEM((n, cg, width), f32),
            pltpu.VMEM((n, cg, width), f32),
            pltpu.VMEM((n, 1, planes), jnp.int32),
            pltpu.SMEM((n, 1, planes), jnp.int32),
            pltpu.VMEM((n * pad, cg, width), f32),
            pltpu.VMEM((n, width), f32),
            pltpu.VMEM((padded, width), f32),
            pltpu.VMEM((padded, width), f32),
            pltpu.VMEM((n, 2 * GROUP, width), f32),
            pltpu.VMEM((owners, 3, LANES), f32),
            pltpu.VMEM((n, 3, LANES), f32),
            pltpu.VMEM((owners, 1, LANES), f32),
            dma,
        ] + [dma((n,)) for _ in range(10)],
        compiler_params=pltpu.CompilerParams(collective_id=0, has_side_effects=True,
                                             vmem_limit_bytes=60 << 20),
    )(features, offsets, conf_bins, plane_depths)


def solution(mesh):
    in_specs = (
        P(("grp", "view"), None, None, None),
        P(("grp", "view"), None),
        P("grp", None),
        P("view"),
    )
    out_specs = (P("view", "grp", None), P("grp", None))
    return jax.shard_map(
        per_device, mesh=mesh, in_specs=in_specs, out_specs=out_specs, check_vma=False
    )
```

```python
import functools

import jax
import jax.numpy as jnp
from jax import lax
from jax.experimental import pallas as pl
from jax.experimental.pallas import tpu as pltpu
from jax.sharding import PartitionSpec as P

ITERS = 4
LANES = 128
GROUP = 8


def shifted(x, amount, lane):
    if amount == 0:
        return x
    return jnp.where(lane >= amount, pltpu.roll(x, amount, 1), 0.0)


def kernel(
    n, feat_ref, off_ref, conf_ref, depth_ref, cost_ref, map_ref,
    feat, xs, xr, offv, offs, table, sqs, spad, part, costs, stat_s, stat_r, res,
    local_sem, xs_send, xs_recv, off_send, off_recv, c_send, c_recv, s_send, s_recv, r_send, r_recv,
):
    _, chans, rows, width = feat_ref.shape
    planes = off_ref.shape[-1]
    owned = depth_ref.shape[0]
    groups = n // rows
    cg = chans // groups
    pad = width // 8
    halo = ITERS
    span = 2 * GROUP
    per_window = GROUP // owned
    windows = planes // GROUP
    blocks = windows + 1
    owners, _, share = stat_s.shape
    parts = width // share
    first_owner = (n - owners) // 2
    me = lax.axis_index("view")
    my_window = me // per_window
    near = max(1, 4 // per_window)
    last_window = my_window // near * near + near - 1

    barrier = pltpu.get_barrier_semaphore()

    def greet(k, carry):
        pl.semaphore_signal(barrier, inc=1, device_id={"view": lax.rem(me + k, n)})
        return carry

    lax.fori_loop(1, n, greet, 0)
    fetch = pltpu.make_async_copy(feat_ref.at[0], feat, local_sem)
    fetch.start()
    offv[me] = off_ref[...]
    fetch.wait()
    for r in range(rows):
        line = feat[:, r, :]
        for g in range(groups):
            xs[r * groups + g] = line[g * cg:(g + 1) * cg]
    pl.semaphore_wait(barrier, n - 1)

    def off_copy(slot, peer):
        return pltpu.make_async_remote_copy(
            src_ref=offv.at[slot], dst_ref=offv.at[slot], send_sem=off_send.at[peer],
            recv_sem=off_recv.at[slot], device_id={"view": peer})

    def feat_copy(slot, peer):
        return pltpu.make_async_remote_copy(
            src_ref=xs.at[peer], dst_ref=xr.at[slot], send_sem=xs_send.at[peer],
            recv_sem=xs_recv.at[slot], device_id={"view": peer})

    def send_feat(k, carry):
        peer = lax.rem(me + k, n)
        off_copy(me, peer).start()
        feat_copy(me, peer).start()
        return carry

    lax.fori_loop(1, n, send_feat, 0)

    lane = lax.broadcasted_iota(jnp.int32, (cg, width), 1)

    def build(view, x):
        for o in range(pad):
            table[view * pad + o] = shifted(x, o, lane)
        sqs[pl.ds(view, 1), :] = jnp.sum(x * x, axis=0, keepdims=True)

    build(me, xs[me])

    def receive(k, carry):
        source = lax.rem(me - k + n, n)
        feat_copy(source, source).wait_recv()
        off_copy(source, source).wait_recv()
        build(source, xr[source])
        return carry

    lax.fori_loop(1, n, receive, 0)

    to_scalar = pltpu.make_async_copy(offv, offs, local_sem)
    to_scalar.start()
    chosen = offv[:, 0, :]
    sq = sqs[...]
    lane_n = lax.broadcasted_iota(jnp.int32, (n, width), 1)
    hot = jnp.concatenate(
        [jnp.where(chosen == o, 1.0, 0.0) for o in range(pad)], axis=0)
    sq_all = jnp.concatenate([shifted(sq, o, lane_n) for o in range(pad)], axis=0)
    hot = hot.T.astype(jnp.bfloat16)
    high = sq_all.astype(jnp.bfloat16)
    rest = sq_all - high.astype(jnp.float32)
    mid = rest.astype(jnp.bfloat16)
    low = (rest - mid.astype(jnp.float32)).astype(jnp.bfloat16)
    square = jnp.zeros((planes, width), jnp.float32)
    for piece in (low, mid, high):
        square = square + jnp.dot(hot, piece, preferred_element_type=jnp.float32)
    spad[...] = jnp.zeros_like(spad)
    spad[halo:halo + planes, :] = square * (1.0 / (n * chans))
    to_scalar.wait()

    def cost_copy(slot, peer, window):
        first = pl.multiple_of(window * GROUP, GROUP)
        return pltpu.make_async_remote_copy(
            src_ref=part.at[pl.ds(first, span)], dst_ref=costs.at[slot],
            send_sem=c_send.at[peer], recv_sem=c_recv.at[slot], device_id={"view": peer})

    def send_cost(window):
        for m in range(per_window):
            peer = window * per_window + m

            @pl.when(peer != me)
            def _():
                cost_copy(me, peer, window).start()

    def block(k, carry):
        j = lax.rem(last_window + 1 + k, blocks)
        sums = []
        for i in range(GROUP):
            p = jnp.clip(j * GROUP + i - halo, 0, planes - 1)
            total = table[offs[0, 0, p]]
            for v in range(1, n):
                total = total + table[v * pad + offs[v, 0, p]]
            sums.append(jnp.sum(total * total, axis=0, keepdims=True))
        first = pl.multiple_of(j * GROUP, GROUP)
        part[pl.ds(first, GROUP), :] = (
            spad[pl.ds(first, GROUP), :]
            - jnp.concatenate(sums, axis=0) * (1.0 / (n * n * chans)))

        @pl.when(jnp.logical_and(k > 0, j > 0))
        def _():
            send_cost(j - 1)

        return carry

    lax.fori_loop(0, blocks, block, 0)
    send_cost(last_window)
    costs[me] = part[pl.ds(pl.multiple_of(my_window * GROUP, GROUP), span), :]

    def take(k, carry):
        source = lax.rem(me - k + n, n)
        cost_copy(source, source, 0).wait_recv()
        return carry

    lax.fori_loop(1, n, take, 0)

    plane = my_window * GROUP - halo + lax.broadcasted_iota(jnp.int32, (span, width), 0)
    valid = jnp.logical_and(plane >= 0, plane < planes)
    col = lax.broadcasted_iota(jnp.int32, (span, width), 1)
    cost, rate = [], []
    for r in range(rows):
        total = costs[r * groups]
        for g in range(1, groups):
            total = total + costs[r * groups + g]
        cost.append(jnp.where(valid, total, 0.0))
        conf = (conf_ref[r:r + 1, :].astype(jnp.float32) + 1.0) * 0.25
        rate.append(jnp.where(valid, 0.15 * conf, 0.0))
    for step in range(ITERS):
        new = []
        for r in range(rows):
            c = cost[r]
            beside = pltpu.roll(c, 1, 0) + pltpu.roll(c, span - 1, 0)
            if r > 0:
                beside = beside + cost[r - 1]
            if r < rows - 1:
                beside = beside + cost[r + 1]
            beside = beside + jnp.where(col > 0, pltpu.roll(c, 1, 1), 0.0)
            beside = beside + jnp.where(col < width - 1, pltpu.roll(c, width - 1, 1), 0.0)
            new.append(c + rate[r] * (beside - 6.0 * c))
        cost = new

    index = lax.broadcasted_iota(jnp.int32, (owned, width), 0)
    depth = jnp.zeros((owned, width), jnp.float32)
    for i in range(owned):
        depth = jnp.where(index == i, depth_ref[i], depth)
    for r in range(rows):
        own = cost[r][halo:halo + owned]
        for m in range(1, per_window):
            first = halo + m * owned
            own = jnp.where(lax.rem(me, per_window) == m, cost[r][first:first + owned], own)
        cost_ref[:, r, :] = own
        peak = jnp.max(-own, axis=0, keepdims=True)
        weight = jnp.exp(-own - peak)
        soft = jnp.concatenate(
            [peak, jnp.sum(weight, axis=0, keepdims=True),
             jnp.sum(weight * depth, axis=0, keepdims=True)], axis=0)
        for h in range(parts):
            stat_s[r * parts + h] = soft[:, h * share:(h + 1) * share]

    mine = me - first_owner
    is_owner = jnp.logical_and(mine >= 0, mine < owners)

    def stat_copy(slot, owner):
        return pltpu.make_async_remote_copy(
            src_ref=stat_s.at[owner], dst_ref=stat_r.at[slot], send_sem=s_send.at[owner],
            recv_sem=s_recv.at[slot], device_id={"view": owner + first_owner})

    def res_copy(owner, peer):
        return pltpu.make_async_remote_copy(
            src_ref=res.at[owner], dst_ref=res.at[owner], send_sem=r_send.at[peer],
            recv_sem=r_recv.at[owner], device_id={"view": peer})

    def send_stat(k, carry):
        owner = lax.rem(me + k, owners)

        @pl.when(owner != mine)
        def _():
            stat_copy(me, owner).start()

        return carry

    lax.fori_loop(0, owners, send_stat, 0)

    @pl.when(is_owner)
    def _():
        stat_r[me] = stat_s[mine]

        def wait_stat(k, carry):
            stat_copy(lax.rem(me - k + n, n), mine).wait_recv()
            return carry

        lax.fori_loop(1, n, wait_stat, 0)
        got = stat_r[...]
        top = jnp.max(got[:, 0, :], axis=0, keepdims=True)
        scale = jnp.exp(got[:, 0, :] - top)
        denom = jnp.sum(got[:, 1, :] * scale, axis=0, keepdims=True)
        numer = jnp.sum(got[:, 2, :] * scale, axis=0, keepdims=True)
        res[mine] = numer / denom

        def send_res(k, carry):
            res_copy(mine, lax.rem(me + k, n)).start()
            return carry

        lax.fori_loop(1, n, send_res, 0)

    def finish(k, carry):
        peer = lax.rem(me + k, n)
        feat_copy(me, peer).wait_send()
        off_copy(me, peer).wait_send()
        cost_copy(me, peer, 0).wait_send()

        @pl.when(is_owner)
        def _():
            res_copy(mine, peer).wait_send()

        return carry

    lax.fori_loop(1, n, finish, 0)

    def collect(owner, carry):
        @pl.when(owner != mine)
        def _():
            stat_copy(me, owner).wait_send()
            res_copy(owner, owner + first_owner).wait_recv()

        return carry

    lax.fori_loop(0, owners, collect, 0)
    for r in range(rows):
        for h in range(parts):
            map_ref[r:r + 1, h * share:(h + 1) * share] = res[r * parts + h]


def per_device(features, offsets, conf_bins, plane_depths):
    n = lax.axis_size("view")
    _, chans, rows, width = features.shape
    planes = offsets.shape[-1]
    owned = plane_depths.shape[0]
    cg = chans * rows // n
    pad = width // 8
    chunks = rows * width // LANES
    share = min(max(1, chunks // max(1, n // 2)) * LANES, width)
    owners = rows * width // share
    padded = planes + 2 * ITERS
    f32 = jnp.float32
    vmem = pl.BlockSpec(memory_space=pltpu.VMEM)
    dma = pltpu.SemaphoreType.DMA
    return pl.pallas_call(
        functools.partial(kernel, n),
        out_shape=(
            jax.ShapeDtypeStruct((owned, rows, width), f32),
            jax.ShapeDtypeStruct((rows, width), f32),
        ),
        in_specs=[pl.BlockSpec(memory_space=pl.ANY), vmem, vmem, pl.BlockSpec(memory_space=pltpu.SMEM)],
        out_specs=(vmem, vmem),
        scratch_shapes=[
            pltpu.VMEM((chans, rows, width), f32),
            pltpu.VMEM((n, cg, width), f32),
            pltpu.VMEM((n, cg, width), f32),
            pltpu.VMEM((n, 1, planes), jnp.int32),
            pltpu.SMEM((n, 1, planes), jnp.int32),
            pltpu.VMEM((n * pad, cg, width), f32),
            pltpu.VMEM((n, width), f32),
            pltpu.VMEM((padded, width), f32),
            pltpu.VMEM((padded, width), f32),
            pltpu.VMEM((n, 2 * GROUP, width), f32),
            pltpu.VMEM((owners, 3, share), f32),
            pltpu.VMEM((n, 3, share), f32),
            pltpu.VMEM((owners, 1, share), f32),
            dma,
        ] + [dma((n,)) for _ in range(10)],
        compiler_params=pltpu.CompilerParams(collective_id=0, has_side_effects=True,
                                             vmem_limit_bytes=60 << 20),
    )(features, offsets, conf_bins, plane_depths)


def solution(mesh):
    in_specs = (
        P(("grp", "view"), None, None, None),
        P(("grp", "view"), None),
        P("grp", None),
        P("view"),
    )
    out_specs = (P("view", "grp", None), P("grp", None))
    return jax.shard_map(
        per_device, mesh=mesh, in_specs=in_specs, out_specs=out_specs, check_vma=False
    )
```

```python
import functools

import jax
import jax.numpy as jnp
from jax import lax
from jax.experimental import pallas as pl
from jax.experimental.pallas import tpu as pltpu
from jax.sharding import PartitionSpec as P

ITERS = 4
LANES = 128
GROUP = 8


def shifted(x, amount, lane):
    if amount == 0:
        return x
    return jnp.where(lane >= amount, pltpu.roll(x, amount, 1), 0.0)


def kernel(
    n, feat_ref, off_ref, conf_ref, depth_ref, cost_ref, map_ref,
    feat, xs, xr, offv, offs, table, sqs, spad, part, costs, stat_s, stat_r, res,
    local_sem, xs_send, xs_recv, off_send, off_recv, c_send, c_recv, s_send, s_recv, r_send, r_recv,
):
    _, chans, rows, width = feat_ref.shape
    planes = off_ref.shape[-1]
    owned = depth_ref.shape[0]
    groups = n // rows
    cg = chans // groups
    pad = width // 8
    halo = ITERS
    span = 2 * GROUP
    per_window = GROUP // owned
    windows = planes // GROUP
    blocks = windows + 1
    owners, _, share = stat_s.shape
    parts = width // share
    first_owner = (n - owners) // 2
    me = lax.axis_index("view")
    my_window = me // per_window
    near = max(1, 4 // per_window)
    last_window = my_window // near * near + near - 1

    barrier = pltpu.get_barrier_semaphore()

    def greet(k, carry):
        pl.semaphore_signal(barrier, inc=1, device_id={"view": lax.rem(me + k, n)})
        return carry

    lax.fori_loop(1, n, greet, 0)
    fetch = pltpu.make_async_copy(feat_ref.at[0], feat, local_sem)
    fetch.start()
    offv[me] = off_ref[...]
    fetch.wait()
    for r in range(rows):
        line = feat[:, r, :]
        for g in range(groups):
            xs[r * groups + g] = line[g * cg:(g + 1) * cg]
    pl.semaphore_wait(barrier, n - 1)

    def off_copy(slot, peer):
        return pltpu.make_async_remote_copy(
            src_ref=offv.at[slot], dst_ref=offv.at[slot], send_sem=off_send.at[peer],
            recv_sem=off_recv.at[slot], device_id={"view": peer})

    def feat_copy(slot, peer):
        return pltpu.make_async_remote_copy(
            src_ref=xs.at[peer], dst_ref=xr.at[slot], send_sem=xs_send.at[peer],
            recv_sem=xs_recv.at[slot], device_id={"view": peer})

    def send_feat(k, carry):
        peer = lax.rem(me + k, n)
        off_copy(me, peer).start()
        feat_copy(me, peer).start()
        return carry

    lax.fori_loop(1, n, send_feat, 0)

    lane = lax.broadcasted_iota(jnp.int32, (cg, width), 1)

    def build(view, x):
        for o in range(pad):
            table[view * pad + o] = shifted(x, o, lane)
        sqs[pl.ds(view, 1), :] = jnp.sum(x * x, axis=0, keepdims=True)

    build(me, xs[me])

    def receive(k, carry):
        source = lax.rem(me - k + n, n)
        feat_copy(source, source).wait_recv()
        off_copy(source, source).wait_recv()
        build(source, xr[source])
        return carry

    lax.fori_loop(1, n, receive, 0)

    to_scalar = pltpu.make_async_copy(offv, offs, local_sem)
    to_scalar.start()
    chosen = offv[:, 0, :]
    sq = sqs[...]
    lane_n = lax.broadcasted_iota(jnp.int32, (n, width), 1)
    hot = jnp.concatenate(
        [jnp.where(chosen == o, 1.0, 0.0) for o in range(pad)], axis=0)
    sq_all = jnp.concatenate([shifted(sq, o, lane_n) for o in range(pad)], axis=0)
    hot = hot.T.astype(jnp.bfloat16)
    high = sq_all.astype(jnp.bfloat16)
    rest = sq_all - high.astype(jnp.float32)
    mid = rest.astype(jnp.bfloat16)
    low = (rest - mid.astype(jnp.float32)).astype(jnp.bfloat16)
    square = jnp.zeros((planes, width), jnp.float32)
    for piece in (low, mid, high):
        square = square + jnp.dot(hot, piece, preferred_element_type=jnp.float32)
    spad[...] = jnp.zeros_like(spad)
    spad[halo:halo + planes, :] = square * (1.0 / (n * chans))
    to_scalar.wait()

    def cost_copy(slot, peer, window):
        first = pl.multiple_of(window * GROUP, GROUP)
        return pltpu.make_async_remote_copy(
            src_ref=part.at[pl.ds(first, span)], dst_ref=costs.at[slot],
            send_sem=c_send.at[peer], recv_sem=c_recv.at[slot], device_id={"view": peer})

    def send_cost(window):
        for m in range(per_window):
            peer = window * per_window + m

            @pl.when(peer != me)
            def _():
                cost_copy(me, peer, window).start()

    def block(k, carry):
        j = lax.rem(last_window + 1 + k, blocks)
        sums = []
        for i in range(GROUP):
            p = jnp.clip(j * GROUP + i - halo, 0, planes - 1)
            total = table[offs[0, 0, p]]
            for v in range(1, n):
                total = total + table[v * pad + offs[v, 0, p]]
            sums.append(jnp.sum(total * total, axis=0, keepdims=True))
        first = pl.multiple_of(j * GROUP, GROUP)
        part[pl.ds(first, GROUP), :] = (
            spad[pl.ds(first, GROUP), :]
            - jnp.concatenate(sums, axis=0) * (1.0 / (n * n * chans)))

        @pl.when(jnp.logical_and(k > 0, j > 0))
        def _():
            send_cost(j - 1)

        return carry

    lax.fori_loop(0, blocks, block, 0)
    send_cost(last_window)
    costs[me] = part[pl.ds(pl.multiple_of(my_window * GROUP, GROUP), span), :]

    def take(k, carry):
        source = lax.rem(me - k + n, n)
        cost_copy(source, source, 0).wait_recv()
        return carry

    lax.fori_loop(1, n, take, 0)

    plane = my_window * GROUP - halo + lax.broadcasted_iota(jnp.int32, (span, width), 0)
    valid = jnp.logical_and(plane >= 0, plane < planes)
    col = lax.broadcasted_iota(jnp.int32, (span, width), 1)
    cost, rate = [], []
    for r in range(rows):
        total = costs[r * groups]
        for g in range(1, groups):
            total = total + costs[r * groups + g]
        cost.append(jnp.where(valid, total, 0.0))
        conf = (conf_ref[r:r + 1, :].astype(jnp.float32) + 1.0) * 0.25
        rate.append(jnp.where(valid, 0.15 * conf, 0.0))
    for step in range(ITERS):
        new = []
        for r in range(rows):
            c = cost[r]
            beside = pltpu.roll(c, 1, 0) + pltpu.roll(c, span - 1, 0)
            if r > 0:
                beside = beside + cost[r - 1]
            if r < rows - 1:
                beside = beside + cost[r + 1]
            beside = beside + jnp.where(col > 0, pltpu.roll(c, 1, 1), 0.0)
            beside = beside + jnp.where(col < width - 1, pltpu.roll(c, width - 1, 1), 0.0)
            new.append(c + rate[r] * (beside - 6.0 * c))
        cost = new

    index = lax.broadcasted_iota(jnp.int32, (owned, width), 0)
    depth = jnp.zeros((owned, width), jnp.float32)
    for i in range(owned):
        depth = jnp.where(index == i, depth_ref[i], depth)
    for r in range(rows):
        own = cost[r][halo:halo + owned]
        for m in range(1, per_window):
            first = halo + m * owned
            own = jnp.where(lax.rem(me, per_window) == m, cost[r][first:first + owned], own)
        cost_ref[:, r, :] = own
        peak = jnp.max(-own, axis=0, keepdims=True)
        weight = jnp.exp(-own - peak)
        soft = jnp.concatenate(
            [peak, jnp.sum(weight, axis=0, keepdims=True),
             jnp.sum(weight * depth, axis=0, keepdims=True)], axis=0)
        for h in range(parts):
            stat_s[r * parts + h] = soft[:, h * share:(h + 1) * share]

    mine = me - first_owner
    is_owner = jnp.logical_and(mine >= 0, mine < owners)

    def stat_copy(slot, owner):
        return pltpu.make_async_remote_copy(
            src_ref=stat_s.at[owner], dst_ref=stat_r.at[slot], send_sem=s_send.at[owner],
            recv_sem=s_recv.at[slot], device_id={"view": owner + first_owner})

    def res_copy(owner, peer):
        return pltpu.make_async_remote_copy(
            src_ref=res.at[owner], dst_ref=res.at[owner], send_sem=r_send.at[peer],
            recv_sem=r_recv.at[owner], device_id={"view": peer})

    def send_stat(k, carry):
        owner = lax.rem(me + k, owners)

        @pl.when(owner != mine)
        def _():
            stat_copy(me, owner).start()

        return carry

    lax.fori_loop(0, owners, send_stat, 0)

    @pl.when(is_owner)
    def _():
        stat_r[me] = stat_s[mine]

        def wait_stat(k, carry):
            stat_copy(lax.rem(me - k + n, n), mine).wait_recv()
            return carry

        lax.fori_loop(1, n, wait_stat, 0)
        got = stat_r[...]
        top = jnp.max(got[:, 0, :], axis=0, keepdims=True)
        scale = jnp.exp(got[:, 0, :] - top)
        denom = jnp.sum(got[:, 1, :] * scale, axis=0, keepdims=True)
        numer = jnp.sum(got[:, 2, :] * scale, axis=0, keepdims=True)
        res[mine] = numer / denom

        def send_res(k, carry):
            res_copy(mine, lax.rem(me + k, n)).start()
            return carry

        lax.fori_loop(1, n, send_res, 0)

    def finish(k, carry):
        peer = lax.rem(me + k, n)
        feat_copy(me, peer).wait_send()
        off_copy(me, peer).wait_send()
        cost_copy(me, peer, 0).wait_send()

        @pl.when(is_owner)
        def _():
            res_copy(mine, peer).wait_send()

        return carry

    lax.fori_loop(1, n, finish, 0)

    def collect(owner, carry):
        @pl.when(owner != mine)
        def _():
            stat_copy(me, owner).wait_send()
            res_copy(owner, owner + first_owner).wait_recv()

        return carry

    lax.fori_loop(0, owners, collect, 0)
    for r in range(rows):
        for h in range(parts):
            map_ref[r:r + 1, h * share:(h + 1) * share] = res[r * parts + h]


def hand_on(cost_in, map_in, cost_out, map_out):
    cost_out[...] = cost_in[...]
    map_out[...] = map_in[...]


def per_device(features, offsets, conf_bins, plane_depths):
    n = lax.axis_size("view")
    _, chans, rows, width = features.shape
    planes = offsets.shape[-1]
    owned = plane_depths.shape[0]
    cg = chans * rows // n
    pad = width // 8
    chunks = rows * width // LANES
    share = min(max(1, chunks // max(1, n // 2)) * LANES, width)
    owners = rows * width // share
    padded = planes + 2 * ITERS
    f32 = jnp.float32
    vmem = pl.BlockSpec(memory_space=pltpu.VMEM)
    dma = pltpu.SemaphoreType.DMA
    outputs = pl.pallas_call(
        functools.partial(kernel, n),
        out_shape=(
            jax.ShapeDtypeStruct((owned, rows, width), f32),
            jax.ShapeDtypeStruct((rows, width), f32),
        ),
        in_specs=[pl.BlockSpec(memory_space=pl.ANY), vmem, vmem, pl.BlockSpec(memory_space=pltpu.SMEM)],
        out_specs=(vmem, vmem),
        scratch_shapes=[
            pltpu.VMEM((chans, rows, width), f32),
            pltpu.VMEM((n, cg, width), f32),
            pltpu.VMEM((n, cg, width), f32),
            pltpu.VMEM((n, 1, planes), jnp.int32),
            pltpu.SMEM((n, 1, planes), jnp.int32),
            pltpu.VMEM((n * pad, cg, width), f32),
            pltpu.VMEM((n, width), f32),
            pltpu.VMEM((padded, width), f32),
            pltpu.VMEM((padded, width), f32),
            pltpu.VMEM((n, 2 * GROUP, width), f32),
            pltpu.VMEM((owners, 3, share), f32),
            pltpu.VMEM((n, 3, share), f32),
            pltpu.VMEM((owners, 1, share), f32),
            dma,
        ] + [dma((n,)) for _ in range(10)],
        compiler_params=pltpu.CompilerParams(collective_id=0, has_side_effects=True,
                                             vmem_limit_bytes=60 << 20),
    )(features, offsets, conf_bins, plane_depths)
    return pl.pallas_call(
        hand_on,
        out_shape=tuple(jax.ShapeDtypeStruct(x.shape, x.dtype) for x in outputs),
        in_specs=[vmem, vmem],
        out_specs=(vmem, vmem),
    )(*outputs)


def solution(mesh):
    in_specs = (
        P(("grp", "view"), None, None, None),
        P(("grp", "view"), None),
        P("grp", None),
        P("view"),
    )
    out_specs = (P("view", "grp", None), P("grp", None))
    return jax.shard_map(
        per_device, mesh=mesh, in_specs=in_specs, out_specs=out_specs, check_vma=False
    )
```
